512 devices in a mesh: space: 128 (over y, z, core), dp: 4 (over x).
Axes of the slice: x: 4, y: 8, z: 8, core: 2. Of those that a mesh axis runs over, the one named last changes fastest.
Arguments:
- features: bfloat16 [4, 65536, 128], P('dp', 'space'), may hold values from -6 to 6
- occupancy: int32 [4, 65536], P('dp', 'space'), may hold values from 0 to 1
- brick_pairs: int32 [4, 1024, 27], P('dp', 'space'), may hold values from 0 to 264, as said below
- send_lists: int32 [4, 128, 256], P('dp', 'space'), may hold values from -1 to 7, as said below
- scan_weight: int32 [4], P('dp'), may hold values from 1 to 12
- kernel: bfloat16 [3456, 128], replicated, may hold values from -0.109375 to 0.109375
- cotangent: bfloat16 [4, 65536, 128], P('dp', 'space'), may hold values from -6 to 6
Outputs:
- output_features: bfloat16 [4, 65536, 128], P('dp', 'space')
- grad_features: bfloat16 [4, 65536, 128], P('dp', 'space')
- grad_kernel: float32 [3456, 128], replicated
The draws below stay inside these ranges and needn't reach their ends.
Inputs may be any that keep to these rules, and one draw needn't show every extreme that they name: `brick_pairs`: entry 13 of brick b is b itself. A value under 8 is a brick of the same owner; 8 + t * 2 + k names entry k of what owner t sends to this owner, and then t differs from this owner's index on space in exactly one bit; 264 is an empty brick. `send_lists`: for a destination t that differs from the owner's index in exactly one bit, 2 distinct slots of the owner; for every other destination all -1.
All inputs are finite; a program needn't handle non-finite values.
Results may differ from the reference program's by a relative error of at most 0.0017.
Values may be sent and summed in bfloat16 or wider, within the bound.
No kernel may reach another device: no remote copies, remote signals or barrier semaphores. Data moves between devices by JAX's collectives and lax.ppermute only.
A program may use at most 64 MiB of HBM per device.

```python
import math
import jax
import jax.numpy as jnp
import numpy as np
from jax import lax

C = 128
BRICK_DEV = 8
PEER_CAP = 2
LEVELS = 7
BRICKS = 1024
N_SPACE = 128
N_DP = 4


def brick_tables(key):
    key_list = jax.random.split(key, 8)
    slot_ids = jnp.arange(BRICK_DEV, dtype=jnp.int32)
    space_ids = jnp.arange(N_SPACE, dtype=jnp.int32)
    live_count = jax.random.randint(key_list[0], (N_DP, N_SPACE), BRICK_DEV // 2, BRICK_DEV + 1)
    live_brick = slot_ids[None, None, :] < live_count[:, :, None]
    thresh = jax.random.randint(key_list[1], (N_DP, N_SPACE, BRICK_DEV, 1), 3, 10)
    coin_toss = jax.random.randint(key_list[2], (N_DP, N_SPACE, BRICK_DEV, 64), 0, 10)
    occupied = jnp.logical_and(coin_toss < thresh, live_brick[:, :, :, None]).astype(jnp.int32)
    sort_score = jax.random.randint(key_list[3], (N_DP, N_SPACE, N_SPACE, BRICK_DEV), 0, 1 << 20) * (2 * BRICK_DEV) + slot_ids + jnp.where(live_brick[:, :, None, :], 0, 1 << 30)
    permuted = jnp.argsort(sort_score, axis=-1)[..., :PEER_CAP].astype(jnp.int32)
    index_gap = jnp.bitwise_xor(space_ids[:, None], space_ids[None, :])
    one_bit = jnp.logical_and(index_gap > 0, jnp.bitwise_and(index_gap, index_gap - 1) == 0)
    send_table = jnp.where(one_bit[None, :, :, None], permuted, -1).reshape(N_DP, N_SPACE, N_SPACE * PEER_CAP).astype(jnp.int32)
    pair_shape = (N_DP, N_SPACE, BRICK_DEV, 27)
    category = jax.random.randint(key_list[4], pair_shape, 0, 10)
    local_pick = jax.random.randint(key_list[5], pair_shape, 0, BRICK_DEV) % live_count[:, :, None, None]
    bit_pick = jax.random.randint(key_list[6], pair_shape, 0, LEVELS)
    slot_pick = jax.random.randint(key_list[7], pair_shape, 0, PEER_CAP)
    partner = jnp.bitwise_xor(space_ids[None, :, None, None], jnp.left_shift(jnp.ones_like(bit_pick), bit_pick))
    zero_index = BRICK_DEV + N_SPACE * PEER_CAP
    neighbour = jnp.where(category < 3, zero_index, jnp.where(category < 6, local_pick, BRICK_DEV + partner * PEER_CAP + slot_pick))
    neighbour = jnp.where(live_brick[:, :, :, None], neighbour, zero_index)
    centre = jnp.broadcast_to(slot_ids[None, None, :, None], pair_shape)
    column_ids = jnp.arange(27, dtype=jnp.int32)
    neighbour = jnp.where(column_ids == 13, centre, neighbour).astype(jnp.int32)
    return (occupied.reshape(N_DP, N_SPACE * BRICK_DEV * 64), neighbour.reshape(N_DP, N_SPACE * BRICK_DEV, 27), send_table)


def draw_occupancy(key, part):
    return brick_tables(jax.random.fold_in(key, 17))[0]


def draw_brick_pairs(key, part):
    return brick_tables(jax.random.fold_in(key, 17))[1]


def draw_send_lists(key, part):
    return brick_tables(jax.random.fold_in(key, 17))[2]


def draw_scan_weight(key, part):
    scan_ids = jnp.arange(N_DP, dtype=jnp.int32)
    raised = jax.random.randint(jax.random.fold_in(key, 29), (N_DP,), 1, 4) + 3 * scan_ids
    return jnp.where(scan_ids == N_DP - 1, 3 * N_DP, raised).astype(jnp.int32)


def block_levels(stream_key, shape, cuts, low, high):
    def one(position, parts):
        draws = jax.random.uniform(jax.random.fold_in(jax.random.fold_in(stream_key, 6), position), (parts,), jnp.float32, low / len(cuts), high / len(cuts))
        return jnp.repeat(jnp.exp(draws), shape[position] // parts).reshape((-1,) + (1,) * (len(shape) - position - 1))

    gain = one(*cuts[0])
    for cut in cuts[1:]:
        gain = gain * one(*cut)
    return gain


def bell_draw(rng, extent, spread, bound, shards=(), kind=jnp.bfloat16):
    factor_of = block_levels(rng, extent, shards, -0.22, 0.18) if shards else 1.0
    entries = jax.random.normal(rng, extent, jnp.float32) * spread * factor_of
    return jnp.minimum(jnp.maximum(entries, -bound), bound).astype(kind)


def setup_inputs(seed: int = 0) -> dict:
    key_of = jax.random.split(jax.random.key(seed), 8)
    return {
        "features": bell_draw(key_of[0], (N_DP, BRICKS * 64, C), 1.0, 6.0, ((0, 4), (1, 128))),
        "occupancy": draw_occupancy(jax.random.fold_in(key_of[7], 71), 0),
        "brick_pairs": draw_brick_pairs(jax.random.fold_in(key_of[7], 71), 0),
        "send_lists": draw_send_lists(jax.random.fold_in(key_of[7], 71), 0),
        "scan_weight": draw_scan_weight(jax.random.fold_in(key_of[7], 71), 0),
        "kernel": bell_draw(key_of[5], (27 * C, C), (27 * C) ** -0.5, 0.109375),
        "cotangent": bell_draw(key_of[6], (N_DP, BRICKS * 64, C), 1.0, 6.0, ((0, 4), (1, 128))),
    }


def patch_layout():
    offset_list = []
    inner_list = []
    for pos_x in range(6):
        for pos_y in range(6):
            for pos_z in range(6):
                offset_parts = []
                inner_parts = []
                for coordinate in (pos_x, pos_y, pos_z):
                    shifted = coordinate - 1
                    brick_step = shifted // 4
                    offset_parts.append(brick_step + 1)
                    inner_parts.append(shifted - 4 * brick_step)
                offset_list.append(9 * offset_parts[0] + 3 * offset_parts[1] + offset_parts[2])
                inner_list.append(16 * inner_parts[0] + 4 * inner_parts[1] + inner_parts[2])
    return (np.array(offset_list, np.int32), np.array(inner_list, np.int32))

def convolve(table_rows, table_index, grad_in, kernel, offset_map, inner_map):
    bricks = table_index.shape[0]
    channels = table_rows.shape[1]
    patch_rows = (table_index[:, offset_map] * 64 + inner_map[None, :]).astype(jnp.int32)
    patch_cube = jnp.take(table_rows, patch_rows.reshape(-1), axis=0).reshape(bricks, 6, 6, 6, channels)
    result = jnp.zeros((bricks * 64, channels), jnp.float32)
    patch_grad = jnp.zeros((bricks, 6, 6, 6, channels), jnp.float32)
    weight_grads = []
    for shift_x in range(3):
        pieces = []
        for tap_index in range(9):
            shift_y = tap_index // 3
            shift_z = tap_index % 3
            pieces.append(patch_cube[:, shift_x:shift_x + 4, shift_y:shift_y + 4, shift_z:shift_z + 4, :].reshape(bricks * 64, channels))
        columns = jnp.concatenate(pieces, axis=1)
        kernel_rows = kernel[shift_x * 9 * channels:(shift_x + 1) * 9 * channels]
        result = result + jnp.dot(columns, kernel_rows, preferred_element_type=jnp.float32)
        weight_grads.append(jnp.dot(columns.T, grad_in, preferred_element_type=jnp.float32))
        for tap_index in range(9):
            shift_y = tap_index // 3
            shift_z = tap_index % 3
            tap_weight = kernel_rows[tap_index * channels:(tap_index + 1) * channels]
            tap_grad = jnp.dot(grad_in, tap_weight.T, preferred_element_type=jnp.float32)
            patch_grad = patch_grad.at[:, shift_x:shift_x + 4, shift_y:shift_y + 4, shift_z:shift_z + 4, :].add(tap_grad.reshape(bricks, 4, 4, 4, channels))
    table_grad = jax.ops.segment_sum(patch_grad.reshape(-1, channels), patch_rows.reshape(-1), num_segments=table_rows.shape[0])
    return (result, table_grad, jnp.concatenate(weight_grads, axis=0))

def halo_index(pair_table, device, bricks, nspace, peer_cap, levels):
    zero_full = bricks + nspace * peer_cap
    relative = jnp.clip(pair_table - bricks, 0, nspace * peer_cap - 1)
    source = relative // peer_cap
    within = relative % peer_cap
    flipped = jnp.bitwise_xor(source, device)
    level_of = jnp.zeros_like(pair_table)
    for bit_level in range(levels):
        level_of = level_of + bit_level * (flipped == 1 << bit_level).astype(jnp.int32)
    compact = bricks + level_of * peer_cap + within
    outside = bricks + levels * peer_cap
    return jnp.where(pair_table < bricks, pair_table, jnp.where(pair_table >= zero_full, outside, compact)).astype(jnp.int32)

def reference(features, occupancy, brick_pairs, send_lists, scan_weight, kernel, cotangent):
    offset_list, inner_list = patch_layout()
    offset_map = jnp.asarray(offset_list, jnp.int32)
    inner_map = jnp.asarray(inner_list, jnp.int32)
    weight_total = jnp.sum(scan_weight.astype(jnp.float32))
    devices = jnp.arange(N_SPACE, dtype=jnp.int32)
    slot_ids = jnp.arange(PEER_CAP, dtype=jnp.int32)
    own_rows = BRICK_DEV * 64
    outputs = []
    feature_grads = []
    kernel_grad = jnp.zeros((27 * C, C), jnp.float32)
    for scan_index in range(N_DP):
        voxel_mask = occupancy[scan_index].reshape(N_SPACE, own_rows, 1).astype(jnp.bfloat16)
        masked = features[scan_index].reshape(N_SPACE, own_rows, C) * voxel_mask
        grad_in = cotangent[scan_index].reshape(N_SPACE, own_rows, C) * voxel_mask
        brick_rows = masked.reshape(N_SPACE, BRICK_DEV, 64 * C)
        send_table = send_lists[scan_index]
        pieces = []
        for bit_level in range(LEVELS):
            partner = jnp.bitwise_xor(devices, 1 << bit_level)
            chosen = send_table[partner[:, None], devices[:, None] * PEER_CAP + slot_ids[None, :]]
            gathered = brick_rows[partner[:, None], jnp.maximum(chosen, 0)]
            pieces.append(jnp.where((chosen >= 0)[:, :, None], gathered, jnp.zeros_like(gathered)))
        empty_brick = jnp.zeros((N_SPACE, 1, 64 * C), jnp.bfloat16)
        brick_table = jnp.concatenate([brick_rows] + pieces + [empty_brick], axis=1).reshape(N_SPACE, -1, C)
        table_index = halo_index(brick_pairs[scan_index].reshape(N_SPACE, BRICK_DEV, 27), devices[:, None, None], BRICK_DEV, N_SPACE, PEER_CAP, LEVELS)

        def per_device(carried, inputs):
            table_rows, device_index, device_grad = inputs
            result, table_grad, weight_grad = convolve(table_rows, device_index, device_grad, kernel, offset_map, inner_map)
            return (carried + weight_grad, (result, table_grad))
        scan_grad, (conv_out, table_grads) = lax.scan(per_device, jnp.zeros((27 * C, C), jnp.float32), (brick_table, table_index, grad_in))
        own_grad = table_grads[:, :own_rows]
        halo_grads = table_grads[:, own_rows:own_rows + LEVELS * PEER_CAP * 64].astype(jnp.bfloat16).reshape(N_SPACE, LEVELS * PEER_CAP, 64 * C)
        collected = jnp.zeros((N_SPACE * BRICK_DEV + 1, 64 * C), jnp.float32)
        for bit_level in range(LEVELS):
            partner = jnp.bitwise_xor(devices, 1 << bit_level)
            grad_piece = halo_grads[partner, bit_level * PEER_CAP:(bit_level + 1) * PEER_CAP]
            chosen = send_table[devices[:, None], partner[:, None] * PEER_CAP + slot_ids[None, :]]
            target = jnp.where(chosen >= 0, devices[:, None] * BRICK_DEV + chosen, N_SPACE * BRICK_DEV).astype(jnp.int32)
            collected = collected + jax.ops.segment_sum(grad_piece.astype(jnp.float32).reshape(-1, 64 * C), target.reshape(-1), num_segments=N_SPACE * BRICK_DEV + 1)
        returned = collected[:-1].reshape(N_SPACE, own_rows, C)
        grad_sum = grad_in.astype(jnp.float32) + own_grad + returned
        factor = scan_weight[scan_index].astype(jnp.float32) * N_DP / weight_total
        mask_float = voxel_mask.astype(jnp.float32)
        outputs.append((mask_float * (conv_out + masked.astype(jnp.float32))).astype(jnp.bfloat16).reshape(N_SPACE * own_rows, C))
        feature_grads.append((factor * (mask_float * grad_sum)).astype(jnp.bfloat16).reshape(N_SPACE * own_rows, C))
        kernel_grad = kernel_grad + factor * scan_grad
    kernel_grad = kernel_grad / math.sqrt(64.0 * BRICKS)
    return (jnp.stack(outputs), jnp.stack(feature_grads), kernel_grad)
```

```python
import math

import jax
import jax.numpy as jnp
import numpy as np
from jax import lax
from jax.sharding import Mesh, PartitionSpec as P


SPACE = ("y", "z", "core")
FULL = 16383.0
FULL_BITS = 14
SHARD_ROWS = 64
SPARE = 16


def bit_axes(sizes):
    steps = []
    for axis in reversed(SPACE):
        for bit in range(sizes[axis].bit_length() - 1):
            steps.append((axis, bit))
    return steps


def swapped(value, step):
    axis, bit = step
    pairs = [(source, source ^ 2**bit) for source in range(lax.axis_size(axis))]
    return lax.ppermute(value, axis, pairs)


def encode(values, extra=None):
    rows = values.shape[-2]
    peak = jnp.max(jnp.abs(values), axis=-2, keepdims=True)
    power = jnp.clip(jnp.ceil(jnp.log2(jnp.maximum(peak, 1e-30))), -100.0, 100.0)
    coded = jnp.round(values * jnp.exp2(FULL_BITS - power)).astype(jnp.int16)
    spare = [power.astype(jnp.int16)]
    if extra is not None:
        spare.append(jnp.broadcast_to(extra.astype(jnp.int16), power.shape))
    fill = -rows % SPARE or SPARE
    spare.append(jnp.zeros(values.shape[:-2] + (fill - len(spare), values.shape[-1]), jnp.int16))
    return jnp.concatenate([coded] + spare, axis=-2)


def decode(coded, rows):
    power = coded[..., rows : rows + 1, :].astype(jnp.float32)
    return coded[..., :rows, :].astype(jnp.float32) * jnp.exp2(power - FULL_BITS)


def exchanged(parts, axes):
    return lax.all_to_all(parts, axes, 0, 0, tiled=True)


def everyone(part, axes, count):
    return exchanged(jnp.broadcast_to(part[None], (count,) + part.shape), axes)


def reduced(weighted, own_weight):
    rows, channels = weighted.shape
    near = ("core", "x")
    near_count = lax.axis_size("core") * lax.axis_size("x")
    depth = lax.axis_size("z")
    breadth = lax.axis_size("y")
    near_rows = rows // near_count
    own_rows = near_rows // depth
    parts = exchanged(encode(weighted.reshape(near_count, near_rows, channels), own_weight), near)
    total_weight = jnp.sum(parts[:, near_rows + 1, 0].astype(jnp.float32)) / lax.axis_size("core")
    part = jnp.sum(decode(parts, near_rows), axis=0)
    parts = exchanged(encode(part.reshape(depth, own_rows, channels)), "z")
    part = jnp.sum(decode(parts, own_rows), axis=0)
    parts = everyone(encode(part), "y", breadth)
    part = jnp.sum(decode(parts, own_rows), axis=0)
    part = decode(everyone(encode(part), "z", depth), own_rows).reshape(near_rows, channels)
    whole = decode(everyone(encode(part), near, near_count), near_rows).reshape(rows, channels)
    return whole, total_weight


def patch_layout():
    offset_list = []
    inner_list = []
    for pos_x in range(6):
        for pos_y in range(6):
            for pos_z in range(6):
                offset_parts = []
                inner_parts = []
                for coordinate in (pos_x, pos_y, pos_z):
                    shifted = coordinate - 1
                    brick_step = shifted // 4
                    offset_parts.append(brick_step + 1)
                    inner_parts.append(shifted - 4 * brick_step)
                offset_list.append(9 * offset_parts[0] + 3 * offset_parts[1] + offset_parts[2])
                inner_list.append(16 * inner_parts[0] + 4 * inner_parts[1] + inner_parts[2])
    return (np.array(offset_list, np.int32), np.array(inner_list, np.int32))


def gradients(table_index, grad_in, kernel, offset_map, inner_map, table_rows):
    bricks = table_index.shape[0]
    channels = grad_in.shape[1]
    patch_rows = table_index[:, offset_map] * 64 + inner_map[None, :]
    patch_grad = jnp.zeros((bricks, 6, 6, 6, channels), jnp.float32)
    for tap in range(27):
        x, y, z = tap // 9, tap // 3 % 3, tap % 3
        tap_weight = kernel[tap * channels : (tap + 1) * channels]
        tap_grad = jnp.dot(grad_in, tap_weight.T, preferred_element_type=jnp.float32)
        patch_grad = patch_grad.at[:, x : x + 4, y : y + 4, z : z + 4, :].add(
            tap_grad.reshape(bricks, 4, 4, 4, channels)
        )
    return jax.ops.segment_sum(
        patch_grad.reshape(-1, channels), patch_rows.reshape(-1), num_segments=table_rows
    )


def convolve(table_rows, table_index, grad_in, kernel, offset_map, inner_map):
    bricks = table_index.shape[0]
    channels = table_rows.shape[1]
    patch_rows = table_index[:, offset_map] * 64 + inner_map[None, :]
    patch_cube = jnp.take(table_rows, patch_rows.reshape(-1), axis=0).reshape(
        bricks, 6, 6, 6, channels
    )
    result = jnp.zeros((bricks * 64, channels), jnp.float32)
    weight_grads = []
    for x in range(3):
        pieces = []
        for tap in range(9):
            y, z = tap // 3, tap % 3
            pieces.append(
                patch_cube[:, x : x + 4, y : y + 4, z : z + 4, :].reshape(bricks * 64, channels)
            )
        columns = jnp.concatenate(pieces, axis=1)
        kernel_rows = kernel[x * 9 * channels : (x + 1) * 9 * channels]
        result = result + jnp.dot(columns, kernel_rows, preferred_element_type=jnp.float32)
        weight_grads.append(jnp.dot(columns.T, grad_in, preferred_element_type=jnp.float32))
    return (result, jnp.concatenate(weight_grads, axis=0))


def halo_index(pair_table, device, bricks, nspace, peer_cap, levels):
    zero_full = bricks + nspace * peer_cap
    relative = jnp.clip(pair_table - bricks, 0, nspace * peer_cap - 1)
    source = relative // peer_cap
    within = relative % peer_cap
    flipped = jnp.bitwise_xor(source, device)
    level_of = jnp.zeros_like(pair_table)
    for bit_level in range(levels):
        level_of = level_of + bit_level * (flipped == 1 << bit_level).astype(jnp.int32)
    compact = bricks + level_of * peer_cap + within
    outside = bricks + levels * peer_cap
    return jnp.where(
        pair_table < bricks, pair_table, jnp.where(pair_table >= zero_full, outside, compact)
    )


def pick_bricks(brick_rows, chosen):
    gathered = jnp.take(brick_rows, jnp.maximum(chosen, 0), axis=0)
    return jnp.where((chosen >= 0)[:, None], gathered, jnp.zeros_like(gathered))


def on_device(features, occupancy, brick_pairs, send_lists, scan_weight, kernel, cotangent):
    offset_list, inner_list = patch_layout()
    offset_map = jnp.asarray(offset_list, jnp.int32)
    inner_map = jnp.asarray(inner_list, jnp.int32)
    channels = features.shape[2]
    own_rows = features.shape[1]
    bricks = own_rows // 64
    nspace = lax.axis_size(SPACE)
    scan_count = lax.axis_size("x")
    steps = bit_axes({axis: lax.axis_size(axis) for axis in SPACE})
    levels = len(steps)
    device = lax.axis_index(SPACE)
    send_table = send_lists[0, 0]
    peer_cap = send_table.shape[0] // nspace
    voxel_mask = occupancy[0][:, None].astype(jnp.bfloat16)
    masked = features[0] * voxel_mask
    grad_in = cotangent[0] * voxel_mask
    brick_rows = masked.reshape(bricks, 64 * channels)
    empty_brick = jnp.zeros((1, 64 * channels), jnp.bfloat16)
    pair_table = brick_pairs[0]
    table_index = halo_index(pair_table, device, bricks, nspace, peer_cap, levels)
    table_grad = gradients(table_index, grad_in, kernel, offset_map, inner_map, (bricks + levels * peer_cap + 1) * 64)
    incoming = []
    returned = jnp.zeros((bricks + 1, 64 * channels), jnp.float32)
    for bit_level in range(levels):
        partner = jnp.bitwise_xor(device, 1 << bit_level)
        chosen = lax.dynamic_slice(send_table, (partner * peer_cap,), (peer_cap,))
        start_row = own_rows + bit_level * peer_cap * 64
        grad_piece = (
            table_grad[start_row : start_row + peer_cap * 64]
            .astype(jnp.bfloat16)
            .reshape(peer_cap, 64 * channels)
        )
        sent = jnp.concatenate([pick_bricks(brick_rows, chosen), grad_piece], axis=0)
        came = swapped(sent, steps[bit_level])
        incoming.append(came[:peer_cap])
        target = jnp.where(chosen >= 0, chosen, bricks)
        returned = returned + jax.ops.segment_sum(
            came[peer_cap:].astype(jnp.float32), target, num_segments=bricks + 1
        )
    brick_table = jnp.concatenate([brick_rows] + incoming + [empty_brick], axis=0).reshape(
        -1, channels
    )
    result, weight_grad = convolve(
        brick_table, table_index, grad_in, kernel, offset_map, inner_map
    )
    returned = returned[:bricks]
    grad_sum = (
        grad_in.astype(jnp.float32) + table_grad[:own_rows] + returned.reshape(own_rows, channels)
    )
    own_weight = scan_weight[0].astype(jnp.float32)
    summed, weight_total = reduced(weight_grad * own_weight, own_weight)
    factor = own_weight * scan_count / weight_total
    mask_float = voxel_mask.astype(jnp.float32)
    output = (mask_float * (result + masked.astype(jnp.float32))).astype(jnp.bfloat16)
    grad_features = (factor * (mask_float * grad_sum)).astype(jnp.bfloat16)
    kernel_grad = summed * (scan_count / weight_total) / math.sqrt(64.0 * bricks * nspace)
    return (output[None], grad_features[None], kernel_grad)


def solution(mesh):
    sizes = dict(mesh.shape)
    assert mesh.axis_names == ("space", "dp")
    inner = Mesh(
        mesh.devices.reshape(8, sizes["space"] // 16, 2, sizes["dp"]), ("y", "z", "core", "x")
    )
    return jax.shard_map(
        on_device,
        mesh=inner,
        in_specs=(
            P("x", SPACE, None),
            P("x", SPACE),
            P("x", SPACE, None),
            P("x", SPACE, None),
            P("x"),
            P(),
            P("x", SPACE, None),
        ),
        out_specs=(P("x", SPACE, None), P("x", SPACE, None), P()),
        check_vma=False,
    )
```

```python
import functools
import math

import jax
import jax.numpy as jnp
from jax import lax
from jax.experimental import pallas as pl
from jax.experimental.pallas import tpu as pltpu
from jax.sharding import Mesh, PartitionSpec as P


SPACE = ("y", "z", "core")
FULL = 16383.0
FULL_BITS = 14
SHARD_ROWS = 64
SPARE = 16


def bit_axes(sizes):
    steps = []
    for axis in reversed(SPACE):
        for bit in range(sizes[axis].bit_length() - 1):
            steps.append((axis, bit))
    return steps


def swapped(value, step):
    axis, bit = step
    pairs = [(source, source ^ 2**bit) for source in range(lax.axis_size(axis))]
    return lax.ppermute(value, axis, pairs)


def encode(values, extra=None):
    rows = values.shape[-2]
    peak = jnp.max(jnp.abs(values), axis=-2, keepdims=True)
    power = jnp.clip(jnp.ceil(jnp.log2(jnp.maximum(peak, 1e-30))), -100.0, 100.0)
    coded = jnp.round(values * jnp.exp2(FULL_BITS - power)).astype(jnp.int16)
    spare = [power.astype(jnp.int16)]
    if extra is not None:
        spare.append(jnp.broadcast_to(extra.astype(jnp.int16), power.shape))
    fill = -rows % SPARE or SPARE
    spare.append(jnp.zeros(values.shape[:-2] + (fill - len(spare), values.shape[-1]), jnp.int16))
    return jnp.concatenate([coded] + spare, axis=-2)


def decode(coded, rows):
    power = coded[..., rows : rows + 1, :].astype(jnp.float32)
    return coded[..., :rows, :].astype(jnp.float32) * jnp.exp2(power - FULL_BITS)


def exchanged(parts, axes):
    return lax.all_to_all(parts, axes, 0, 0, tiled=True)


def everyone(part, axes, count):
    return exchanged(jnp.broadcast_to(part[None], (count,) + part.shape), axes)


def reduced(weighted, own_weight):
    rows, channels = weighted.shape
    near = ("core", "x")
    near_count = lax.axis_size("core") * lax.axis_size("x")
    depth = lax.axis_size("z")
    breadth = lax.axis_size("y")
    near_rows = rows // near_count
    own_rows = near_rows // depth
    parts = exchanged(encode(weighted.reshape(near_count, near_rows, channels), own_weight), near)
    total_weight = jnp.sum(parts[:, near_rows + 1, 0].astype(jnp.float32)) / lax.axis_size("core")
    part = jnp.sum(decode(parts, near_rows), axis=0)
    parts = exchanged(encode(part.reshape(depth, own_rows, channels)), "z")
    part = jnp.sum(decode(parts, own_rows), axis=0)
    parts = everyone(encode(part), "y", breadth)
    part = jnp.sum(decode(parts, own_rows), axis=0)
    part = decode(everyone(encode(part), "z", depth), own_rows).reshape(near_rows, channels)
    whole = decode(everyone(encode(part), near, near_count), near_rows).reshape(rows, channels)
    return whole, total_weight


def halo_place(pair_table, device, bricks, nspace, peer_cap, levels):
    relative = jnp.clip(pair_table - bricks, 0, nspace * peer_cap - 1)
    flipped = jnp.bitwise_xor(relative // peer_cap, device)
    level_of = jnp.zeros_like(pair_table)
    for bit_level in range(levels):
        level_of = level_of + bit_level * (flipped == 1 << bit_level).astype(jnp.int32)
    kind = jnp.where(
        pair_table < bricks, 0, jnp.where(pair_table >= bricks + nspace * peer_cap, 2, 1)
    )
    return kind, level_of, relative % peer_cap


def voxel_sources():
    sources = []
    for pos in range(6):
        step = (pos - 1) // 4
        sources.append((step + 1, pos - 1 - 4 * step))
    return sources


SOURCES = voxel_sources()


def onehot(left, right, dtype=jnp.bfloat16):
    return jnp.where(left == right, 1.0, 0.0).astype(dtype)


def stacked_rows(rows):
    channels = rows.shape[1] // 64
    return jnp.concatenate(
        [
            rows[:, (xy * 4 + z) * channels : (xy * 4 + z + 1) * channels]
            for z in range(4)
            for xy in range(16)
        ],
        axis=0,
    )


def backward_kernel(levels, grad_ref, own_ref, kernel_ref, rows_ref, pick_ref, *refs):
    send_refs = refs[:levels]
    own_grad_ref, cube_ref, table_ref = refs[levels:]
    bricks = grad_ref.shape[0]
    channels = kernel_ref.shape[1]
    wide = 4 * channels
    grad = grad_ref[...].astype(jnp.float32)
    stacked = stacked_rows(grad).astype(jnp.bfloat16)
    cube_ref[...] = jnp.zeros_like(cube_ref)
    for tap in range(9):
        tap_x, tap_y = tap // 3, tap % 3
        weight = kernel_ref[tap * 3 * channels : (tap + 1) * 3 * channels, :]
        part = lax.dot_general(
            stacked, weight, (((1,), (1,)), ((), ())), preferred_element_type=jnp.float32
        )
        for z in range(4):
            for x in range(4):
                for y in range(4):
                    row = (z * 16 + x * 4 + y) * bricks
                    cube_ref[
                        (x + tap_x) * 6 + y + tap_y, :, z * channels : (z + 3) * channels
                    ] += part[row : row + bricks]
    table_rows = table_ref.shape[0]
    slots = lax.broadcasted_iota(jnp.int32, (table_rows, 2 * bricks), 0)
    chooser = [
        onehot(slots, jnp.broadcast_to(rows_ref[offset : offset + 1, :], slots.shape))
        for offset in range(27)
    ]
    for xy in range(16):
        total = None
        low = None
        high = None
        for pos_x in range(6):
            for pos_y in range(6):
                if (SOURCES[pos_x][1], SOURCES[pos_y][1]) != (xy // 4, xy % 4):
                    continue
                base = 9 * SOURCES[pos_x][0] + 3 * SOURCES[pos_y][0]
                piece = cube_ref[pos_x * 6 + pos_y]
                upper = piece.astype(jnp.bfloat16)
                lower = (piece - upper.astype(jnp.float32)).astype(jnp.bfloat16)
                both = jnp.concatenate([upper, lower], axis=0)

                def spread(offset, start, stop):
                    return jnp.dot(
                        chooser[offset], both[:, start:stop], preferred_element_type=jnp.float32
                    )

                mid = spread(base + 1, channels, 5 * channels)
                first = spread(base + 2, 5 * channels, 6 * channels)
                last = spread(base, 0, channels)
                total = mid if total is None else total + mid
                low = first if low is None else low + first
                high = last if high is None else high + last
        start = xy * wide
        table_ref[:, start : start + channels] = total[:, :channels] + low
        table_ref[:, start + channels : start + 3 * channels] = total[:, channels : 3 * channels]
        table_ref[:, start + 3 * channels : start + wide] = total[:, 3 * channels :] + high
    pick_rows = pick_ref.shape[0]
    lanes = lax.broadcasted_iota(jnp.int32, (pick_rows, bricks), 1)
    picker = onehot(lanes, jnp.broadcast_to(pick_ref[...], lanes.shape))
    for xy in range(16):
        span = slice(xy * wide, (xy + 1) * wide)
        sent = table_ref[:pick_rows, span] + jnp.dot(
            picker, own_ref[:, span], preferred_element_type=jnp.float32
        )
        for level in range(levels):
            send_refs[level][:, span] = sent[4 * level : 4 * level + 4].astype(jnp.bfloat16)
        own_grad_ref[:, span] = table_ref[pick_rows:, span] + grad[:, span]


def patch_kernel(table_ref, grad_ref, rows_ref, weight_ref, cube_ref):
    bricks = grad_ref.shape[0]
    table_rows = table_ref.shape[0]
    channels = weight_ref.shape[1]
    wide = 4 * channels
    lanes = lax.broadcasted_iota(jnp.int32, (27 * bricks, table_rows), 1)
    chooser = onehot(lanes, jnp.broadcast_to(rows_ref[...], lanes.shape), jnp.float32)
    for xy in range(16):
        places = [
            (pos_x, pos_y)
            for pos_x in range(6)
            for pos_y in range(6)
            if (SOURCES[pos_x][1], SOURCES[pos_y][1]) == (xy // 4, xy % 4)
        ]

        def picked(side, start, stop):
            rows = []
            for pos_x, pos_y in places:
                offset = 9 * SOURCES[pos_x][0] + 3 * SOURCES[pos_y][0] + side
                rows.append(chooser[offset * bricks : (offset + 1) * bricks])
            rows = rows[0] if len(rows) == 1 else jnp.concatenate(rows, axis=0)
            return jnp.dot(
                rows.astype(jnp.bfloat16),
                table_ref[:, xy * wide + start : xy * wide + stop],
                preferred_element_type=jnp.float32,
            )

        first = picked(0, 3 * channels, wide)
        mid = picked(1, 0, wide)
        last = picked(2, 0, channels)
        for at, (pos_x, pos_y) in enumerate(places):
            rows = slice(at * bricks, (at + 1) * bricks)
            cube_ref[pos_x * 6 + pos_y, :, :channels] = first[rows]
            cube_ref[pos_x * 6 + pos_y, :, channels : 5 * channels] = mid[rows]
            cube_ref[pos_x * 6 + pos_y, :, 5 * channels :] = last[rows]
    turned = stacked_rows(grad_ref[...].astype(jnp.float32)).T.astype(jnp.bfloat16)
    for tap in range(9):
        part = jnp.dot(turned, columns_of(cube_ref, tap), preferred_element_type=jnp.float32)
        for tap_z in range(3):
            row = (tap * 3 + tap_z) * channels
            weight_ref[row : row + channels, :] = part[:, tap_z * channels : (tap_z + 1) * channels].T


def columns_of(cube_ref, tap):
    channels = cube_ref.shape[2] // 6
    tap_x, tap_y = tap // 3, tap % 3
    slab = jnp.concatenate(
        [cube_ref[(x + tap_x) * 6 + y + tap_y] for x in range(4) for y in range(4)], axis=0
    ).astype(jnp.bfloat16)
    return jnp.concatenate(
        [slab[:, z * channels : (z + 3) * channels] for z in range(4)], axis=0
    )


def forward_kernel(
    cube_ref, kernel_ref, table_ref, own_ref, own_grad_ref, back_ref, mask_ref, out_ref, sum_ref
):
    bricks = own_ref.shape[0]
    channels = kernel_ref.shape[1]
    total = None
    for tap in range(9):
        part = jnp.dot(
            columns_of(cube_ref, tap),
            kernel_ref[tap * 3 * channels : (tap + 1) * 3 * channels, :],
            preferred_element_type=jnp.float32,
        )
        total = part if total is None else total + part
    owners = lax.broadcasted_iota(jnp.int32, (bricks, table_ref.shape[0]), 0)
    backer = onehot(owners, jnp.broadcast_to(back_ref[...], owners.shape))
    for xy in range(16):
        for z in range(4):
            voxel = xy * 4 + z
            span = slice(voxel * channels, (voxel + 1) * channels)
            row = (z * 16 + xy) * bricks
            mask = jnp.broadcast_to(mask_ref[:, voxel : voxel + 1], (bricks, channels))
            own = own_ref[:, span].astype(jnp.float32)
            out_ref[:, span] = (mask * (total[row : row + bricks] + own)).astype(jnp.bfloat16)
            back = jnp.dot(backer, table_ref[:, span], preferred_element_type=jnp.float32)
            sum_ref[:, span] = mask * (own_grad_ref[:, span] + back)


def local_call(body, out_shape, scratch, flops, moved):
    return pl.pallas_call(
        body,
        out_shape=out_shape,
        scratch_shapes=scratch,
        compiler_params=pltpu.CompilerParams(vmem_limit_bytes=40 * 1024 * 1024),
        cost_estimate=pl.CostEstimate(flops=flops, bytes_accessed=moved, transcendentals=0),
    )


def on_device(features, occupancy, brick_pairs, send_lists, scan_weight, kernel, cotangent):
    channels = features.shape[2]
    own_rows = features.shape[1]
    bricks = own_rows // 64
    nspace = lax.axis_size(SPACE)
    scan_count = lax.axis_size("x")
    steps = bit_axes({axis: lax.axis_size(axis) for axis in SPACE})
    levels = len(steps)
    device = lax.axis_index(SPACE)
    send_table = send_lists[0, 0]
    peer_cap = send_table.shape[0] // nspace
    assert peer_cap == 2 and bricks == 8
    send_rows = -(-4 * levels // 8) * 8
    table_rows = send_rows + bricks
    width = 64 * channels
    voxel_mask = occupancy[0][:, None].astype(jnp.bfloat16)
    masked = (features[0] * voxel_mask).reshape(bricks, width)
    grad_in = (cotangent[0] * voxel_mask).reshape(bricks, width)
    mask_float = occupancy[0].reshape(bricks, 64).astype(jnp.float32)
    kind, level_of, within = halo_place(brick_pairs[0].T, device, bricks, nspace, peer_cap, levels)
    pair_table = brick_pairs[0].T
    forward_rows = jnp.where(
        kind == 0, send_rows + pair_table, jnp.where(kind == 1, 4 * level_of + within, -1)
    )
    backward_rows = jnp.where(kind == 1, forward_rows + peer_cap, forward_rows)
    backward_rows = jnp.concatenate([backward_rows, backward_rows], axis=1)
    forward_rows = forward_rows.reshape(27 * bricks, 1)
    partners = jnp.bitwise_xor(device, jnp.left_shift(1, jnp.arange(levels, dtype=jnp.int32)))
    entries = partners[:, None] * peer_cap + jnp.arange(peer_cap, dtype=jnp.int32)[None, :]
    chosen = jnp.take(send_table, entries.reshape(-1)).reshape(levels, peer_cap)
    nothing = jnp.full((levels, peer_cap), -1, jnp.int32)
    pick_rows = jnp.pad(
        jnp.concatenate([chosen, nothing], axis=1).reshape(-1),
        (0, send_rows - 4 * levels),
        constant_values=-1,
    ).reshape(send_rows, 1)
    back_rows = jnp.pad(
        jnp.concatenate([nothing, chosen], axis=1).reshape(-1),
        (0, table_rows - 4 * levels),
        constant_values=-1,
    ).reshape(1, table_rows)
    macs = own_rows * 27 * channels * channels
    cube = (36, bricks, 6 * channels)
    *sends, own_grad = local_call(
        functools.partial(backward_kernel, levels),
        [jax.ShapeDtypeStruct((4, width), jnp.bfloat16)] * levels
        + [jax.ShapeDtypeStruct((bricks, width), jnp.float32)],
        [pltpu.VMEM(cube, jnp.float32), pltpu.VMEM((table_rows, width), jnp.float32)],
        2 * macs,
        4 * 2**20,
    )(grad_in, masked, kernel, backward_rows, pick_rows)
    came = [swapped(sends[level], steps[level]) for level in range(levels)]
    blank = jnp.zeros((send_rows - 4 * levels, width), jnp.bfloat16)
    table = jnp.concatenate(came + [blank, masked], axis=0)
    weight_grad, cubes = local_call(
        patch_kernel,
        [
            jax.ShapeDtypeStruct(kernel.shape, jnp.float32),
            jax.ShapeDtypeStruct(cube, jnp.float32),
        ],
        [],
        2 * macs,
        4 * 2**20,
    )(table, grad_in, forward_rows)
    output, grad_sum = local_call(
        forward_kernel,
        [
            jax.ShapeDtypeStruct((bricks, width), jnp.bfloat16),
            jax.ShapeDtypeStruct((bricks, width), jnp.float32),
        ],
        [],
        2 * macs,
        4 * 2**20,
    )(cubes, kernel, table, masked, own_grad, back_rows, mask_float)
    own_weight = scan_weight[0].astype(jnp.float32)
    summed, weight_total = reduced(weight_grad * own_weight, own_weight)
    factor = own_weight * scan_count / weight_total
    grad_features = (factor * grad_sum).astype(jnp.bfloat16)
    kernel_grad = summed * (scan_count / weight_total) / math.sqrt(64.0 * bricks * nspace)
    return (
        output.reshape(1, own_rows, channels),
        grad_features.reshape(1, own_rows, channels),
        kernel_grad,
    )


def solution(mesh):
    sizes = dict(mesh.shape)
    assert mesh.axis_names == ("space", "dp")
    inner = Mesh(
        mesh.devices.reshape(8, sizes["space"] // 16, 2, sizes["dp"]), ("y", "z", "core", "x")
    )
    return jax.shard_map(
        on_device,
        mesh=inner,
        in_specs=(
            P("x", SPACE, None),
            P("x", SPACE),
            P("x", SPACE, None),
            P("x", SPACE, None),
            P("x"),
            P(),
            P("x", SPACE, None),
        ),
        out_specs=(P("x", SPACE, None), P("x", SPACE, None), P()),
        check_vma=False,
    )
```

```python
import functools
import math

import jax
import jax.numpy as jnp
from jax import lax
from jax.experimental import pallas as pl
from jax.experimental.pallas import tpu as pltpu
from jax.sharding import Mesh, PartitionSpec as P


SPACE = ("y", "z", "core")
FULL_BITS = 14


def bit_axes(sizes):
    steps = []
    for axis in reversed(SPACE):
        for bit in range(sizes[axis].bit_length() - 1):
            steps.append((axis, bit))
    return steps


def swapped(value, step):
    axis, bit = step
    pairs = [(source, source ^ 2**bit) for source in range(lax.axis_size(axis))]
    return lax.ppermute(value, axis, pairs)


def encoded(values, rows, weight=None):
    have = values.shape[0]
    peak = jnp.max(jnp.abs(values), axis=0, keepdims=True)
    power = jnp.clip(jnp.ceil(jnp.log2(jnp.maximum(peak, 1e-30))), -100.0, 100.0)
    coded = jnp.round(values * jnp.exp2(FULL_BITS - power))
    spare = (rows - have, values.shape[1])
    place = lax.broadcasted_iota(jnp.int32, spare, 0)
    extra = jnp.where(place == 0, jnp.broadcast_to(power, spare), 0.0)
    if weight is not None:
        extra = jnp.where(place == 1, weight, extra)
    return jnp.concatenate([coded, extra], axis=0).astype(jnp.int32).astype(jnp.int16)


def decoded(coded, have):
    values = coded.astype(jnp.int32).astype(jnp.float32)
    return values[:have] * jnp.exp2(values[have : have + 1] - FULL_BITS), values[have + 1 : have + 2]


def near_kernel(have, copies, coded_ref, out_ref, total_ref):
    summed = None
    weights = None
    for source in range(coded_ref.shape[0]):
        values, weight = decoded(coded_ref[source], have)
        values = values * weight
        summed = values if summed is None else summed + values
        weights = weight if weights is None else weights + weight
    channels = summed.shape[1]
    depth, rows, _ = out_ref.shape
    step = rows - 8
    summed = jnp.concatenate(
        [summed, jnp.zeros((depth * step - have, channels), jnp.float32)], axis=0
    )
    for target in range(depth):
        out_ref[target] = encoded(summed[target * step : (target + 1) * step], rows)
    total_ref[...] = jnp.broadcast_to(weights * (1.0 / copies), total_ref.shape)


def far_kernel(coded_ref, out_ref):
    rows = coded_ref.shape[1]
    summed = None
    for source in range(coded_ref.shape[0]):
        values, _ = decoded(coded_ref[source], rows - 8)
        summed = values if summed is None else summed + values
    code = encoded(summed, rows)
    for target in range(out_ref.shape[0]):
        out_ref[target] = code


def joined_kernel(have, coded_ref, out_ref):
    rows = coded_ref.shape[1]
    parts = [decoded(coded_ref[source], rows - 8)[0] for source in range(coded_ref.shape[0])]
    code = encoded(jnp.concatenate(parts, axis=0)[:have], out_ref.shape[1])
    for target in range(out_ref.shape[0]):
        out_ref[target] = code


def final_kernel(have, scale, coded_ref, total_ref, out_ref):
    factor = scale / total_ref[0:1, :]
    for source in range(coded_ref.shape[0]):
        values, _ = decoded(coded_ref[source], have)
        out_ref[source * have : (source + 1) * have, :] = values * factor


def exchanged(parts, axes):
    return lax.all_to_all(parts, axes, 0, 0, tiled=True)


def reduced(coded, rows, scale):
    near_count, near_rows, channels = coded.shape
    have = rows // near_count
    near = ("core", "x")
    depth = lax.axis_size("z")
    breadth = lax.axis_size("y")
    far_rows = -(-have // (8 * depth)) * 8 + 8
    passed = jax.ShapeDtypeStruct((depth, far_rows, channels), jnp.int16)
    spread = jax.ShapeDtypeStruct((breadth, far_rows, channels), jnp.int16)
    part, total = local_call(
        functools.partial(near_kernel, have, lax.axis_size("core")),
        [passed, jax.ShapeDtypeStruct((8, channels), jnp.float32)],
        [],
        rows * channels * 4,
        2 * rows * channels,
    )(exchanged(coded, near))
    small = depth * far_rows * channels
    part = local_call(far_kernel, spread, [], small, 2 * small)(exchanged(part, "z"))
    part = local_call(far_kernel, passed, [], small, 2 * small)(exchanged(part, "y"))
    whole = local_call(
        functools.partial(joined_kernel, have),
        jax.ShapeDtypeStruct(coded.shape, jnp.int16),
        [],
        small,
        2 * rows * channels,
    )(exchanged(part, "z"))
    result = local_call(
        functools.partial(final_kernel, have, scale),
        jax.ShapeDtypeStruct((rows, channels), jnp.float32),
        [],
        rows * channels * 4,
        6 * rows * channels,
    )(exchanged(whole, near), total)
    return result, total


def halo_place(pair_table, device, bricks, nspace, peer_cap, levels):
    relative = jnp.clip(pair_table - bricks, 0, nspace * peer_cap - 1)
    flipped = jnp.bitwise_xor(relative // peer_cap, device)
    level_of = jnp.zeros_like(pair_table)
    for bit_level in range(levels):
        level_of = level_of + bit_level * (flipped == 1 << bit_level).astype(jnp.int32)
    kind = jnp.where(
        pair_table < bricks, 0, jnp.where(pair_table >= bricks + nspace * peer_cap, 2, 1)
    )
    return kind, level_of, relative % peer_cap


def voxel_sources():
    sources = []
    for pos in range(6):
        step = (pos - 1) // 4
        sources.append((step + 1, pos - 1 - 4 * step))
    return sources


SOURCES = voxel_sources()


def onehot(left, right, dtype=jnp.bfloat16):
    return jnp.where(left == right, 1.0, 0.0).astype(dtype)


def voxel_rows(natural_ref, bricks):
    return [
        natural_ref[pl.ds(voxel, bricks, stride=64), :] for voxel in range(64)
    ]


def stacked_rows(rows):
    channels = rows.shape[1] // 64
    return jnp.concatenate(
        [
            rows[:, (xy * 4 + z) * channels : (xy * 4 + z + 1) * channels]
            for z in range(4)
            for xy in range(16)
        ],
        axis=0,
    )


def backward_kernel(
    levels, feature_ref, cotangent_ref, mask_ref, kernel_ref, rows_ref, pick_ref, *refs
):
    send_refs = refs[:levels]
    own_grad_ref, own_ref, grad_ref, cube_ref, table_ref, natural_ref = refs[levels:]
    bricks = mask_ref.shape[0]
    channels = kernel_ref.shape[1]
    wide = 4 * channels
    masks = [
        jnp.broadcast_to(mask_ref[:, voxel : voxel + 1], (bricks, channels)) for voxel in range(64)
    ]
    natural_ref[0] = cotangent_ref[...].astype(jnp.float32)
    natural_ref[1] = feature_ref[...].astype(jnp.float32)
    grads = [
        rows * mask for rows, mask in zip(voxel_rows(natural_ref.at[0], bricks), masks)
    ]
    owns = [rows * mask for rows, mask in zip(voxel_rows(natural_ref.at[1], bricks), masks)]
    grad = jnp.concatenate(grads, axis=1)
    grad_ref[...] = grad.astype(jnp.bfloat16)
    own_ref[...] = jnp.concatenate(owns, axis=1).astype(jnp.bfloat16)
    stacked = stacked_rows(grad).astype(jnp.bfloat16)
    cube_ref[...] = jnp.zeros_like(cube_ref)
    for tap in range(9):
        tap_x, tap_y = tap // 3, tap % 3
        weight = kernel_ref[tap * 3 * channels : (tap + 1) * 3 * channels, :]
        part = lax.dot_general(
            stacked, weight, (((1,), (1,)), ((), ())), preferred_element_type=jnp.float32
        )
        for z in range(4):
            for x in range(4):
                for y in range(4):
                    row = (z * 16 + x * 4 + y) * bricks
                    cube_ref[
                        (x + tap_x) * 6 + y + tap_y, :, z * channels : (z + 3) * channels
                    ] += part[row : row + bricks]
    table_rows = table_ref.shape[0]
    slots = lax.broadcasted_iota(jnp.int32, (table_rows, 2 * bricks), 0)
    chooser = [
        onehot(slots, jnp.broadcast_to(rows_ref[offset : offset + 1, :], slots.shape))
        for offset in range(27)
    ]
    for xy in range(16):
        total = None
        low = None
        high = None
        for pos_x in range(6):
            for pos_y in range(6):
                if (SOURCES[pos_x][1], SOURCES[pos_y][1]) != (xy // 4, xy % 4):
                    continue
                base = 9 * SOURCES[pos_x][0] + 3 * SOURCES[pos_y][0]
                piece = cube_ref[pos_x * 6 + pos_y]
                upper = piece.astype(jnp.bfloat16)
                lower = (piece - upper.astype(jnp.float32)).astype(jnp.bfloat16)
                both = jnp.concatenate([upper, lower], axis=0)

                def spread(offset, start, stop):
                    return jnp.dot(
                        chooser[offset], both[:, start:stop], preferred_element_type=jnp.float32
                    )

                mid = spread(base + 1, channels, 5 * channels)
                first = spread(base + 2, 5 * channels, 6 * channels)
                last = spread(base, 0, channels)
                total = mid if total is None else total + mid
                low = first if low is None else low + first
                high = last if high is None else high + last
        start = xy * wide
        table_ref[:, start : start + channels] = total[:, :channels] + low
        table_ref[:, start + channels : start + 3 * channels] = total[:, channels : 3 * channels]
        table_ref[:, start + 3 * channels : start + wide] = total[:, 3 * channels :] + high
    pick_rows = pick_ref.shape[0]
    lanes = lax.broadcasted_iota(jnp.int32, (pick_rows, bricks), 1)
    picker = onehot(lanes, jnp.broadcast_to(pick_ref[...], lanes.shape))
    for xy in range(16):
        span = slice(xy * wide, (xy + 1) * wide)
        sent = table_ref[:pick_rows, span] + jnp.dot(
            picker, own_ref[:, span], preferred_element_type=jnp.float32
        )
        for level in range(levels):
            send_refs[level][:, span] = sent[4 * level : 4 * level + 4].astype(jnp.bfloat16)
        own_grad_ref[:, span] = table_ref[pick_rows:, span] + grad[:, span]


def patch_kernel(table_ref, grad_ref, rows_ref, scan_ref, code_ref, cube_ref, weight_ref):
    bricks = grad_ref.shape[0]
    table_rows = table_ref.shape[0]
    channels = weight_ref.shape[1]
    wide = 4 * channels
    lanes = lax.broadcasted_iota(jnp.int32, (27 * bricks, table_rows), 1)
    chooser = onehot(lanes, jnp.broadcast_to(rows_ref[...], lanes.shape), jnp.float32)
    for xy in range(16):
        places = [
            (pos_x, pos_y)
            for pos_x in range(6)
            for pos_y in range(6)
            if (SOURCES[pos_x][1], SOURCES[pos_y][1]) == (xy // 4, xy % 4)
        ]

        def picked(side, start, stop):
            rows = []
            for pos_x, pos_y in places:
                offset = 9 * SOURCES[pos_x][0] + 3 * SOURCES[pos_y][0] + side
                rows.append(chooser[offset * bricks : (offset + 1) * bricks])
            rows = rows[0] if len(rows) == 1 else jnp.concatenate(rows, axis=0)
            return jnp.dot(
                rows.astype(jnp.bfloat16),
                table_ref[:, xy * wide + start : xy * wide + stop],
                preferred_element_type=jnp.float32,
            )

        first = picked(0, 3 * channels, wide)
        mid = picked(1, 0, wide)
        last = picked(2, 0, channels)
        for at, (pos_x, pos_y) in enumerate(places):
            rows = slice(at * bricks, (at + 1) * bricks)
            cube_ref[pos_x * 6 + pos_y, :, :channels] = first[rows]
            cube_ref[pos_x * 6 + pos_y, :, channels : 5 * channels] = mid[rows]
            cube_ref[pos_x * 6 + pos_y, :, 5 * channels :] = last[rows]
    turned = stacked_rows(grad_ref[...].astype(jnp.float32)).T.astype(jnp.bfloat16)
    for tap in range(9):
        part = jnp.dot(turned, columns_of(cube_ref, tap), preferred_element_type=jnp.float32)
        for tap_z in range(3):
            row = (tap * 3 + tap_z) * channels
            weight_ref[row : row + channels, :] = part[:, tap_z * channels : (tap_z + 1) * channels].T
    own_weight = scan_ref[0].astype(jnp.float32)
    near_count, near_rows, _ = code_ref.shape
    have = weight_ref.shape[0] // near_count
    for target in range(near_count):
        code_ref[target] = encoded(
            weight_ref[target * have : (target + 1) * have, :], near_rows, own_weight
        )


def columns_of(cube_ref, tap):
    channels = cube_ref.shape[2] // 6
    tap_x, tap_y = tap // 3, tap % 3
    slab = jnp.concatenate(
        [cube_ref[(x + tap_x) * 6 + y + tap_y] for x in range(4) for y in range(4)], axis=0
    ).astype(jnp.bfloat16)
    return jnp.concatenate(
        [slab[:, z * channels : (z + 3) * channels] for z in range(4)], axis=0
    )


def forward_kernel(
    scans,
    cube_ref,
    kernel_ref,
    table_ref,
    own_ref,
    own_grad_ref,
    back_ref,
    mask_ref,
    scan_ref,
    total_ref,
    out_ref,
    sum_ref,
    natural_ref,
):
    bricks = own_ref.shape[0]
    channels = kernel_ref.shape[1]
    total = None
    for tap in range(9):
        part = jnp.dot(
            columns_of(cube_ref, tap),
            kernel_ref[tap * 3 * channels : (tap + 1) * 3 * channels, :],
            preferred_element_type=jnp.float32,
        )
        total = part if total is None else total + part
    owners = lax.broadcasted_iota(jnp.int32, (bricks, table_ref.shape[0]), 0)
    backer = onehot(owners, jnp.broadcast_to(back_ref[...], owners.shape))
    factor = jnp.broadcast_to(
        scan_ref[0].astype(jnp.float32) * scans / total_ref[0:1, :], (bricks, channels)
    )
    for xy in range(16):
        back = jnp.dot(
            backer,
            table_ref[:, xy * 4 * channels : (xy + 1) * 4 * channels],
            preferred_element_type=jnp.float32,
        )
        for z in range(4):
            voxel = xy * 4 + z
            span = slice(voxel * channels, (voxel + 1) * channels)
            row = (z * 16 + xy) * bricks
            mask = jnp.broadcast_to(mask_ref[:, voxel : voxel + 1], (bricks, channels))
            own = own_ref[:, span].astype(jnp.float32)
            lines = pl.ds(voxel, bricks, stride=64)
            natural_ref[0, lines, :] = mask * (total[row : row + bricks] + own)
            grads = own_grad_ref[:, span] + back[:, z * channels : (z + 1) * channels]
            natural_ref[1, lines, :] = factor * (mask * grads)
    out_ref[...] = natural_ref[0].astype(jnp.bfloat16)
    sum_ref[...] = natural_ref[1].astype(jnp.bfloat16)


def local_call(body, out_shape, scratch, flops, moved, in_specs=None):
    keys = {} if in_specs is None else {"in_specs": in_specs}
    return pl.pallas_call(
        body,
        out_shape=out_shape,
        **keys,
        scratch_shapes=scratch,
        compiler_params=pltpu.CompilerParams(vmem_limit_bytes=40 * 1024 * 1024),
        cost_estimate=pl.CostEstimate(flops=flops, bytes_accessed=moved, transcendentals=0),
    )


def on_device(features, occupancy, brick_pairs, send_lists, scan_weight, kernel, cotangent):
    channels = features.shape[2]
    own_rows = features.shape[1]
    bricks = own_rows // 64
    nspace = lax.axis_size(SPACE)
    scan_count = lax.axis_size("x")
    steps = bit_axes({axis: lax.axis_size(axis) for axis in SPACE})
    levels = len(steps)
    device = lax.axis_index(SPACE)
    send_table = send_lists[0, 0]
    peer_cap = send_table.shape[0] // nspace
    assert peer_cap == 2 and bricks == 8
    send_rows = -(-4 * levels // 8) * 8
    table_rows = send_rows + bricks
    width = 64 * channels
    mask_float = occupancy[0].reshape(bricks, 64).astype(jnp.float32)
    kind, level_of, within = halo_place(brick_pairs[0].T, device, bricks, nspace, peer_cap, levels)
    pair_table = brick_pairs[0].T
    forward_rows = jnp.where(
        kind == 0, send_rows + pair_table, jnp.where(kind == 1, 4 * level_of + within, -1)
    )
    backward_rows = jnp.where(kind == 1, forward_rows + peer_cap, forward_rows)
    backward_rows = jnp.concatenate([backward_rows, backward_rows], axis=1)
    forward_rows = forward_rows.reshape(27 * bricks, 1)
    partners = jnp.bitwise_xor(device, jnp.left_shift(1, jnp.arange(levels, dtype=jnp.int32)))
    entries = partners[:, None] * peer_cap + jnp.arange(peer_cap, dtype=jnp.int32)[None, :]
    chosen = jnp.take(send_table, entries.reshape(-1)).reshape(levels, peer_cap)
    nothing = jnp.full((levels, peer_cap), -1, jnp.int32)
    pick_rows = jnp.pad(
        jnp.concatenate([chosen, nothing], axis=1).reshape(-1),
        (0, send_rows - 4 * levels),
        constant_values=-1,
    ).reshape(send_rows, 1)
    back_rows = jnp.pad(
        jnp.concatenate([nothing, chosen], axis=1).reshape(-1),
        (0, table_rows - 4 * levels),
        constant_values=-1,
    ).reshape(1, table_rows)
    macs = own_rows * 27 * channels * channels
    cube = (36, bricks, 6 * channels)
    rowed = jax.ShapeDtypeStruct((bricks, width), jnp.bfloat16)
    plain = jax.ShapeDtypeStruct((own_rows, channels), jnp.bfloat16)
    natural = pltpu.VMEM((2, own_rows, channels), jnp.float32)
    *sends, own_grad, masked, grad_in = local_call(
        functools.partial(backward_kernel, levels),
        [jax.ShapeDtypeStruct((4, width), jnp.bfloat16)] * levels
        + [jax.ShapeDtypeStruct((bricks, width), jnp.float32), rowed, rowed],
        [pltpu.VMEM(cube, jnp.float32), pltpu.VMEM((table_rows, width), jnp.float32), natural],
        2 * macs,
        4 * 2**20,
    )(features[0], cotangent[0], mask_float, kernel, backward_rows, pick_rows)
    came = [swapped(sends[level], steps[level]) for level in range(levels)]
    blank = jnp.zeros((send_rows - 4 * levels, width), jnp.bfloat16)
    table = jnp.concatenate(came + [blank, masked], axis=0)
    near_count = lax.axis_size("core") * lax.axis_size("x")
    near_rows = kernel.shape[0] // near_count + 16
    scalar = pl.BlockSpec(memory_space=pltpu.SMEM)
    whole = pl.BlockSpec(memory_space=pltpu.VMEM)
    coded, cubes = local_call(
        patch_kernel,
        [
            jax.ShapeDtypeStruct((near_count, near_rows, channels), jnp.int16),
            jax.ShapeDtypeStruct(cube, jnp.float32),
        ],
        [pltpu.VMEM(kernel.shape, jnp.float32)],
        2 * macs,
        4 * 2**20,
        [whole] * 3 + [scalar],
    )(table, grad_in, forward_rows, scan_weight)
    scale = scan_count / math.sqrt(64.0 * bricks * nspace)
    kernel_grad, weight_total = reduced(coded, kernel.shape[0], scale)
    output, grad_features = local_call(
        functools.partial(forward_kernel, float(scan_count)),
        [plain, plain],
        [natural],
        2 * macs,
        4 * 2**20,
        [whole] * 7 + [scalar, whole],
    )(cubes, kernel, table, masked, own_grad, back_rows, mask_float, scan_weight, weight_total)
    return (output[None], grad_features[None], kernel_grad)


def solution(mesh):
    sizes = dict(mesh.shape)
    assert mesh.axis_names == ("space", "dp")
    inner = Mesh(
        mesh.devices.reshape(8, sizes["space"] // 16, 2, sizes["dp"]), ("y", "z", "core", "x")
    )
    return jax.shard_map(
        on_device,
        mesh=inner,
        in_specs=(
            P("x", SPACE, None),
            P("x", SPACE),
            P("x", SPACE, None),
            P("x", SPACE, None),
            P("x"),
            P(),
            P("x", SPACE, None),
        ),
        out_specs=(P("x", SPACE, None), P("x", SPACE, None), P()),
        check_vma=False,
    )
```

```python
import functools
import math

import jax
import jax.numpy as jnp
from jax import lax
from jax.experimental import pallas as pl
from jax.experimental.pallas import tpu as pltpu
from jax.sharding import Mesh, PartitionSpec as P


SPACE = ("y", "z", "core")
FULL_BITS = 14


def bit_axes(sizes):
    steps = []
    for axis in reversed(SPACE):
        for bit in range(sizes[axis].bit_length() - 1):
            steps.append((axis, bit))
    return steps


def swapped(value, step):
    axis, bit = step
    pairs = [(source, source ^ 2**bit) for source in range(lax.axis_size(axis))]
    return lax.ppermute(value, axis, pairs)


def encoded(values, rows, weight=None):
    have = values.shape[0]
    peak = jnp.max(jnp.abs(values), axis=0, keepdims=True)
    power = jnp.clip(jnp.ceil(jnp.log2(jnp.maximum(peak, 1e-30))), -100.0, 100.0)
    coded = jnp.round(values * jnp.exp2(FULL_BITS - power))
    spare = (rows - have, values.shape[1])
    place = lax.broadcasted_iota(jnp.int32, spare, 0)
    extra = jnp.where(place == 0, jnp.broadcast_to(power, spare), 0.0)
    if weight is not None:
        extra = jnp.where(place == 1, weight, extra)
    return jnp.concatenate([coded, extra], axis=0).astype(jnp.int32).astype(jnp.int16)


def decoded(coded, have):
    values = coded.astype(jnp.int32).astype(jnp.float32)
    return values[:have] * jnp.exp2(values[have : have + 1] - FULL_BITS), values[have + 1 : have + 2]


def near_kernel(have, copies, coded_ref, out_ref, total_ref):
    summed = None
    weights = None
    for source in range(coded_ref.shape[0]):
        values, weight = decoded(coded_ref[source], have)
        values = values * weight
        summed = values if summed is None else summed + values
        weights = weight if weights is None else weights + weight
    channels = summed.shape[1]
    depth, rows, _ = out_ref.shape
    step = rows - 8
    summed = jnp.concatenate(
        [summed, jnp.zeros((depth * step - have, channels), jnp.float32)], axis=0
    )
    for target in range(depth):
        out_ref[target] = encoded(summed[target * step : (target + 1) * step], rows)
    total_ref[...] = jnp.broadcast_to(weights * (1.0 / copies), total_ref.shape)


def far_kernel(coded_ref, out_ref):
    rows = coded_ref.shape[1]
    summed = None
    for source in range(coded_ref.shape[0]):
        values, _ = decoded(coded_ref[source], rows - 8)
        summed = values if summed is None else summed + values
    code = encoded(summed, rows)
    for target in range(out_ref.shape[0]):
        out_ref[target] = code


def joined_kernel(have, coded_ref, out_ref):
    rows = coded_ref.shape[1]
    parts = [decoded(coded_ref[source], rows - 8)[0] for source in range(coded_ref.shape[0])]
    code = encoded(jnp.concatenate(parts, axis=0)[:have], out_ref.shape[1])
    for target in range(out_ref.shape[0]):
        out_ref[target] = code


def final_kernel(have, scale, coded_ref, total_ref, out_ref):
    factor = scale / total_ref[0:1, :]
    for source in range(coded_ref.shape[0]):
        values, _ = decoded(coded_ref[source], have)
        out_ref[source * have : (source + 1) * have, :] = values * factor


def exchanged(parts, axes):
    return lax.all_to_all(parts, axes, 0, 0, tiled=True)


def reduced(coded, rows, scale):
    near_count, _, channels = coded.shape
    have = rows // near_count
    near = ("core", "x")
    depth = lax.axis_size("z")
    breadth = lax.axis_size("y")
    far_rows = -(-have // (8 * depth)) * 8 + 8
    passed = jax.ShapeDtypeStruct((depth, far_rows, channels), jnp.int16)
    spread = jax.ShapeDtypeStruct((breadth, far_rows, channels), jnp.int16)
    part, total = local_call(
        functools.partial(near_kernel, have, lax.axis_size("core")),
        [passed, jax.ShapeDtypeStruct((8, channels), jnp.float32)],
        [],
        rows * channels * 4,
        2 * rows * channels,
    )(exchanged(coded, near))
    small = depth * far_rows * channels
    part = local_call(far_kernel, spread, [], small, 2 * small)(exchanged(part, "z"))
    part = local_call(far_kernel, passed, [], small, 2 * small)(exchanged(part, "y"))
    whole = local_call(
        functools.partial(joined_kernel, have),
        jax.ShapeDtypeStruct(coded.shape, jnp.int16),
        [],
        small,
        2 * rows * channels,
    )(exchanged(part, "z"))
    result = local_call(
        functools.partial(final_kernel, have, scale),
        jax.ShapeDtypeStruct((rows, channels), jnp.float32),
        [],
        rows * channels * 4,
        6 * rows * channels,
    )(exchanged(whole, near), total)
    return result, total


def halo_place(pair_table, device, bricks, nspace, peer_cap, levels):
    relative = jnp.clip(pair_table - bricks, 0, nspace * peer_cap - 1)
    flipped = jnp.bitwise_xor(lax.div(relative, peer_cap), device)
    level_of = jnp.zeros_like(pair_table)
    for bit_level in range(levels):
        level_of = level_of + bit_level * (flipped == 1 << bit_level).astype(jnp.int32)
    kind = jnp.where(
        pair_table < bricks, 0, jnp.where(pair_table >= bricks + nspace * peer_cap, 2, 1)
    )
    return kind, level_of, lax.rem(relative, peer_cap)


def voxel_sources():
    sources = []
    for pos in range(6):
        step = (pos - 1) // 4
        sources.append((step + 1, pos - 1 - 4 * step))
    return sources


SOURCES = voxel_sources()


def onehot(left, right, dtype=jnp.bfloat16):
    return jnp.where(left == right, 1.0, 0.0).astype(dtype)


def voxel_rows(natural_ref, bricks):
    return [
        natural_ref[pl.ds(voxel, bricks, stride=64), :] for voxel in range(64)
    ]


def stacked_rows(rows):
    channels = rows.shape[1] // 64
    return jnp.concatenate(
        [
            rows[:, (xy * 4 + z) * channels : (xy * 4 + z + 1) * channels]
            for z in range(4)
            for xy in range(16)
        ],
        axis=0,
    )


def backward_kernel(
    levels,
    peer_cap,
    feature_hbm,
    cotangent_hbm,
    kernel_hbm,
    occupancy_hbm,
    pair_hbm,
    send_hbm,
    *refs,
):
    send_refs = refs[:levels]
    own_grad_ref, own_ref, grad_ref, mask_ref, forward_ref, backer_ref = refs[levels : levels + 6]
    cube_ref, table_ref, natural_ref, *staged, copy_sems = refs[levels + 6 :]
    feature_ref, cotangent_ref, kernel_ref, occupancy_ref, pair_ref, list_ref = staged
    sources = (feature_hbm, cotangent_hbm, kernel_hbm, occupancy_hbm, pair_hbm, send_hbm)
    copies = [
        pltpu.make_async_copy(source, target, copy_sems.at[at])
        for at, (source, target) in enumerate(zip(sources, staged))
    ]
    for copy in copies:
        copy.start()
    cube_ref[...] = jnp.zeros_like(cube_ref)
    bricks = mask_ref.shape[0]
    channels = kernel_ref.shape[1]
    wide = 4 * channels
    table_rows = table_ref.shape[0]
    pick_rows = table_rows - bricks
    for copy in copies:
        copy.wait()
    device = lax.axis_index(SPACE)
    occupancy = occupancy_ref[...].astype(jnp.float32)
    mask = jnp.concatenate(
        [occupancy[:, 64 * brick : 64 * brick + 64] for brick in range(bricks)], axis=0
    )
    mask_ref[...] = mask
    pairs = pair_ref[...]
    kind, level_of, within = halo_place(
        pairs, device, bricks, list_ref.shape[1] // peer_cap, peer_cap, levels
    )
    forward = jnp.where(
        kind == 0, pick_rows + pairs, jnp.where(kind == 1, 4 * level_of + within, -1)
    )
    forward_ref[...] = forward
    backward = jnp.where(kind == 1, forward + peer_cap, forward).astype(jnp.float32)
    turned = jnp.concatenate(
        [backward, jnp.zeros((bricks, 128 - backward.shape[1]), jnp.float32)], axis=1
    ).T.astype(jnp.int32)
    turned = jnp.concatenate([turned, turned], axis=1)
    pick_row = lax.broadcasted_iota(jnp.int32, (pick_rows, bricks), 0)
    pick_lane = lax.broadcasted_iota(jnp.int32, (pick_rows, bricks), 1)
    back_row = lax.broadcasted_iota(jnp.int32, (bricks, table_rows), 0)
    back_lane = lax.broadcasted_iota(jnp.int32, (bricks, table_rows), 1)
    picker = jnp.zeros(pick_row.shape, jnp.float32)
    backer = jnp.zeros(back_row.shape, jnp.float32)
    for level in range(levels):
        partner = jnp.bitwise_xor(device, 1 << level)
        for entry in range(peer_cap):
            chosen = list_ref[0, partner * peer_cap + entry]
            at_pick = jnp.logical_and(pick_row == 4 * level + entry, pick_lane == chosen)
            at_back = jnp.logical_and(
                back_lane == 4 * level + peer_cap + entry, back_row == chosen
            )
            picker = jnp.where(at_pick, 1.0, picker)
            backer = jnp.where(at_back, 1.0, backer)
    picker = picker.astype(jnp.bfloat16)
    backer_ref[...] = backer.astype(jnp.bfloat16)
    masks = [
        jnp.broadcast_to(mask[:, voxel : voxel + 1], (bricks, channels)) for voxel in range(64)
    ]
    natural_ref[0] = cotangent_ref[...].astype(jnp.float32)
    natural_ref[1] = feature_ref[...].astype(jnp.float32)
    grads = [
        rows * mask for rows, mask in zip(voxel_rows(natural_ref.at[0], bricks), masks)
    ]
    owns = [rows * mask for rows, mask in zip(voxel_rows(natural_ref.at[1], bricks), masks)]
    grad = jnp.concatenate(grads, axis=1)
    grad_ref[...] = grad.astype(jnp.bfloat16)
    own_ref[...] = jnp.concatenate(owns, axis=1).astype(jnp.bfloat16)
    stacked = stacked_rows(grad).astype(jnp.bfloat16)
    for tap in range(9):
        tap_x, tap_y = tap // 3, tap % 3
        weight = kernel_ref[tap * 3 * channels : (tap + 1) * 3 * channels, :]
        part = lax.dot_general(
            stacked, weight, (((1,), (1,)), ((), ())), preferred_element_type=jnp.float32
        )
        for z in range(4):
            for x in range(4):
                for y in range(4):
                    row = (z * 16 + x * 4 + y) * bricks
                    cube_ref[
                        (x + tap_x) * 6 + y + tap_y, :, z * channels : (z + 3) * channels
                    ] += part[row : row + bricks]
    slots = lax.broadcasted_iota(jnp.int32, (table_rows, 2 * bricks), 0)
    chooser = [
        onehot(slots, jnp.broadcast_to(turned[offset : offset + 1, :], slots.shape))
        for offset in range(27)
    ]
    for xy in range(16):
        total = None
        low = None
        high = None
        for pos_x in range(6):
            for pos_y in range(6):
                if (SOURCES[pos_x][1], SOURCES[pos_y][1]) != (xy // 4, xy % 4):
                    continue
                base = 9 * SOURCES[pos_x][0] + 3 * SOURCES[pos_y][0]
                piece = cube_ref[pos_x * 6 + pos_y]
                upper = piece.astype(jnp.bfloat16)
                lower = (piece - upper.astype(jnp.float32)).astype(jnp.bfloat16)
                both = jnp.concatenate([upper, lower], axis=0)

                def spread(offset, start, stop):
                    return jnp.dot(
                        chooser[offset], both[:, start:stop], preferred_element_type=jnp.float32
                    )

                mid = spread(base + 1, channels, 5 * channels)
                first = spread(base + 2, 5 * channels, 6 * channels)
                last = spread(base, 0, channels)
                total = mid if total is None else total + mid
                low = first if low is None else low + first
                high = last if high is None else high + last
        start = xy * wide
        table_ref[:, start : start + channels] = total[:, :channels] + low
        table_ref[:, start + channels : start + 3 * channels] = total[:, channels : 3 * channels]
        table_ref[:, start + 3 * channels : start + wide] = total[:, 3 * channels :] + high
    for xy in range(16):
        span = slice(xy * wide, (xy + 1) * wide)
        sent = table_ref[:pick_rows, span] + jnp.dot(
            picker, own_ref[:, span], preferred_element_type=jnp.float32
        )
        for level in range(levels):
            send_refs[level][:, span] = sent[4 * level : 4 * level + 4].astype(jnp.bfloat16)
        own_grad_ref[:, span] = table_ref[pick_rows:, span] + grad[:, span]


def patch_kernel(table_ref, grad_ref, rows_ref, scan_ref, code_ref, cube_ref, weight_ref):
    bricks = grad_ref.shape[0]
    table_rows = table_ref.shape[0]
    channels = weight_ref.shape[1]
    wide = 4 * channels
    lanes = lax.broadcasted_iota(jnp.int32, (bricks, table_rows), 1)
    chooser = [
        onehot(
            lanes, jnp.broadcast_to(rows_ref[:, offset : offset + 1], lanes.shape), jnp.float32
        )
        for offset in range(27)
    ]
    for xy in range(16):
        places = [
            (pos_x, pos_y)
            for pos_x in range(6)
            for pos_y in range(6)
            if (SOURCES[pos_x][1], SOURCES[pos_y][1]) == (xy // 4, xy % 4)
        ]

        def picked(side, start, stop):
            rows = []
            for pos_x, pos_y in places:
                offset = 9 * SOURCES[pos_x][0] + 3 * SOURCES[pos_y][0] + side
                rows.append(chooser[offset])
            rows = rows[0] if len(rows) == 1 else jnp.concatenate(rows, axis=0)
            return jnp.dot(
                rows.astype(jnp.bfloat16),
                table_ref[:, xy * wide + start : xy * wide + stop],
                preferred_element_type=jnp.float32,
            )

        first = picked(0, 3 * channels, wide)
        mid = picked(1, 0, wide)
        last = picked(2, 0, channels)
        for at, (pos_x, pos_y) in enumerate(places):
            rows = slice(at * bricks, (at + 1) * bricks)
            cube_ref[pos_x * 6 + pos_y, :, :channels] = first[rows]
            cube_ref[pos_x * 6 + pos_y, :, channels : 5 * channels] = mid[rows]
            cube_ref[pos_x * 6 + pos_y, :, 5 * channels :] = last[rows]
    turned = stacked_rows(grad_ref[...].astype(jnp.float32)).T.astype(jnp.bfloat16)
    for tap in range(9):
        part = jnp.dot(turned, columns_of(cube_ref, tap), preferred_element_type=jnp.float32)
        for tap_z in range(3):
            row = (tap * 3 + tap_z) * channels
            weight_ref[row : row + channels, :] = part[:, tap_z * channels : (tap_z + 1) * channels].T
    own_weight = scan_ref[0].astype(jnp.float32)
    near_count, near_rows, _ = code_ref.shape
    have = weight_ref.shape[0] // near_count
    for target in range(near_count):
        code_ref[target] = encoded(
            weight_ref[target * have : (target + 1) * have, :], near_rows, own_weight
        )


def columns_of(cube_ref, tap):
    channels = cube_ref.shape[2] // 6
    tap_x, tap_y = tap // 3, tap % 3
    slab = jnp.concatenate(
        [cube_ref[(x + tap_x) * 6 + y + tap_y] for x in range(4) for y in range(4)], axis=0
    ).astype(jnp.bfloat16)
    return jnp.concatenate(
        [slab[:, z * channels : (z + 3) * channels] for z in range(4)], axis=0
    )


def forward_kernel(
    scans,
    cube_ref,
    kernel_ref,
    table_ref,
    own_ref,
    own_grad_ref,
    back_ref,
    mask_ref,
    scan_ref,
    total_ref,
    out_ref,
    sum_ref,
    natural_ref,
):
    bricks = own_ref.shape[0]
    channels = kernel_ref.shape[1]
    total = None
    for tap in range(9):
        part = jnp.dot(
            columns_of(cube_ref, tap),
            kernel_ref[tap * 3 * channels : (tap + 1) * 3 * channels, :],
            preferred_element_type=jnp.float32,
        )
        total = part if total is None else total + part
    backer = back_ref[...]
    factor = jnp.broadcast_to(
        scan_ref[0].astype(jnp.float32) * scans / total_ref[0:1, :], (bricks, channels)
    )
    for xy in range(16):
        back = jnp.dot(
            backer,
            table_ref[:, xy * 4 * channels : (xy + 1) * 4 * channels],
            preferred_element_type=jnp.float32,
        )
        for z in range(4):
            voxel = xy * 4 + z
            span = slice(voxel * channels, (voxel + 1) * channels)
            row = (z * 16 + xy) * bricks
            mask = jnp.broadcast_to(mask_ref[:, voxel : voxel + 1], (bricks, channels))
            own = own_ref[:, span].astype(jnp.float32)
            lines = pl.ds(voxel, bricks, stride=64)
            natural_ref[0, lines, :] = mask * (total[row : row + bricks] + own)
            grads = own_grad_ref[:, span] + back[:, z * channels : (z + 1) * channels]
            natural_ref[1, lines, :] = factor * (mask * grads)
    out_ref[...] = natural_ref[0].astype(jnp.bfloat16)
    sum_ref[...] = natural_ref[1].astype(jnp.bfloat16)


def local_call(body, out_shape, scratch, flops, moved, in_specs=None):
    keys = {} if in_specs is None else {"in_specs": in_specs}
    return pl.pallas_call(
        body,
        out_shape=out_shape,
        **keys,
        scratch_shapes=scratch,
        compiler_params=pltpu.CompilerParams(vmem_limit_bytes=40 * 1024 * 1024),
        cost_estimate=pl.CostEstimate(flops=flops, bytes_accessed=moved, transcendentals=0),
    )


def on_device(features, occupancy, brick_pairs, send_lists, scan_weight, kernel, cotangent):
    channels = features.shape[2]
    own_rows = features.shape[1]
    bricks = own_rows // 64
    nspace = lax.axis_size(SPACE)
    scan_count = lax.axis_size("x")
    steps = bit_axes({axis: lax.axis_size(axis) for axis in SPACE})
    levels = len(steps)
    peer_cap = send_lists.shape[2] // nspace
    assert peer_cap == 2 and bricks == 8
    send_rows = -(-4 * levels // 8) * 8
    table_rows = send_rows + bricks
    width = 64 * channels
    macs = own_rows * 27 * channels * channels
    cube = (36, bricks, 6 * channels)
    rowed = jax.ShapeDtypeStruct((bricks, width), jnp.bfloat16)
    plain = jax.ShapeDtypeStruct((own_rows, channels), jnp.bfloat16)
    natural = pltpu.VMEM((2, own_rows, channels), jnp.float32)
    *sends, own_grad, masked, grad_in, mask, forward_rows, backer = local_call(
        functools.partial(backward_kernel, levels, peer_cap),
        [jax.ShapeDtypeStruct((4, width), jnp.bfloat16)] * levels
        + [
            jax.ShapeDtypeStruct((bricks, width), jnp.float32),
            rowed,
            rowed,
            jax.ShapeDtypeStruct((bricks, 64), jnp.float32),
            jax.ShapeDtypeStruct((bricks, 27), jnp.int32),
            jax.ShapeDtypeStruct((bricks, table_rows), jnp.bfloat16),
        ],
        [
            pltpu.VMEM(cube, jnp.float32),
            pltpu.VMEM((table_rows, width), jnp.float32),
            natural,
            pltpu.VMEM((own_rows, channels), jnp.bfloat16),
            pltpu.VMEM((own_rows, channels), jnp.bfloat16),
            pltpu.VMEM(kernel.shape, jnp.bfloat16),
            pltpu.VMEM((1, own_rows), jnp.int32),
            pltpu.VMEM((bricks, 27), jnp.int32),
            pltpu.SMEM((1, send_lists.shape[2]), jnp.int32),
            pltpu.SemaphoreType.DMA((6,)),
        ],
        2 * macs,
        4 * 2**20,
        [pl.BlockSpec(memory_space=pl.ANY)] * 6,
    )(features[0], cotangent[0], kernel, occupancy, brick_pairs[0], send_lists[0])
    came = [None] * levels
    for level in range(levels):
        came[level] = swapped(sends[level], steps[level])
    blank = jnp.zeros((send_rows - 4 * levels, width), jnp.bfloat16)
    table = jnp.concatenate(came + [blank, masked], axis=0)
    near_count = lax.axis_size("core") * lax.axis_size("x")
    near_rows = kernel.shape[0] // near_count + 16
    scalar = pl.BlockSpec(memory_space=pltpu.SMEM)
    whole = pl.BlockSpec(memory_space=pltpu.VMEM)
    coded, cubes = local_call(
        patch_kernel,
        [
            jax.ShapeDtypeStruct((near_count, near_rows, channels), jnp.int16),
            jax.ShapeDtypeStruct(cube, jnp.float32),
        ],
        [pltpu.VMEM(kernel.shape, jnp.float32)],
        2 * macs,
        4 * 2**20,
        [whole] * 3 + [scalar],
    )(table, grad_in, forward_rows, scan_weight)
    scale = scan_count / math.sqrt(64.0 * bricks * nspace)
    kernel_grad, weight_total = reduced(coded, kernel.shape[0], scale)
    output, grad_features = local_call(
        functools.partial(forward_kernel, float(scan_count)),
        [plain, plain],
        [natural],
        2 * macs,
        4 * 2**20,
        [whole] * 7 + [scalar, whole],
    )(cubes, kernel, table, masked, own_grad, backer, mask, scan_weight, weight_total)
    return (output[None], grad_features[None], kernel_grad)


def solution(mesh):
    sizes = dict(mesh.shape)
    assert mesh.axis_names == ("space", "dp")
    inner = Mesh(
        mesh.devices.reshape(8, sizes["space"] // 16, 2, sizes["dp"]), ("y", "z", "core", "x")
    )
    return jax.shard_map(
        on_device,
        mesh=inner,
        in_specs=(
            P("x", SPACE, None),
            P("x", SPACE),
            P("x", SPACE, None),
            P("x", SPACE, None),
            P("x"),
            P(),
            P("x", SPACE, None),
        ),
        out_specs=(P("x", SPACE, None), P("x", SPACE, None), P()),
        check_vma=False,
    )
```
